32 devices in a mesh: groups: 2 (over y), branch: 2 (over core), dap: 4 (over z), tile: 2 (over x).
Axes of the slice: x: 2, y: 2, z: 4, core: 2. Of those that a mesh axis runs over, the one named last changes fastest.
Arguments:
- homolog_hidden: bfloat16 [64, 256, 256], P(('groups', 'dap'), ('branch', 'tile')), parts along dimension 0, may hold values from -6 to 6
- duo_hidden: bfloat16 [512, 256, 128], P(('groups', 'branch', 'tile'), 'dap'), parts along dimension 0, may hold values from -6 to 6
- homolog_valid_flags: int32 [64, 256], P(('groups', 'dap'), ('branch', 'tile')), parts along dimension 0, may hold values 0 or 1
- duo_valid_flags: int32 [512, 256], P(('groups', 'branch', 'tile'), 'dap'), parts along dimension 0, may hold values 0 or 1
- polymer_labeling: int32 [512], P('groups'), parts along dimension 0, may hold values from 0 to 3, never falling along the last dimension, each value on 1 to 128 neighbouring positions
- monomer_serials: int32 [512], P('groups'), parts along dimension 0, may hold values from 0 to 510, as said below
- separation_bin_vectors: bfloat16 [66, 128], replicated, may hold values from -4 to 4
- duo_logit_rescale: float32 [128], replicated, may hold values from 0.25 to 1.75
- duo_logit_projector: bfloat16 [128, 8], replicated, may hold values from -0.5 to 0.5
- homolog_heeded_rescale: float32 [256], replicated, may hold values from 0.25 to 1.75
- qkv_valve_projectors: bfloat16 [256, 1024], replicated
- heeded_exit_projector: bfloat16 [256, 256], replicated, may hold values from -0.375 to 0.375
- dyadic_rescale: float32 [256], replicated, may hold values from 0.25 to 1.75
- dyadic_factor_projector: bfloat16 [256, 64], replicated, may hold values from -0.375 to 0.375
- dyadic_exit_projector: bfloat16 [1024, 128], replicated, may hold values from -1.5 to 1.5
- triad_entry_rescales: float32 [2, 128], replicated, may hold values from 0.25 to 1.75
- triad_entry_projectors: bfloat16 [2, 128, 512], replicated, may hold values from -0.5 to 0.5
- triad_valve_projectors: bfloat16 [2, 128, 128], replicated, may hold values from -0.5 to 0.5
- triad_exit_rescales: float32 [2, 128], replicated, may hold values from 0.25 to 1.75
- triad_exit_projectors: bfloat16 [2, 128, 128], replicated, may hold values from -0.5 to 0.5
Outputs:
- lineup_updated_state: bfloat16 [64, 256, 256], P(('groups', 'dap'), ('branch', 'tile')), parts along dimension 0
- pair_out: bfloat16 [512, 256, 128], P(('groups', 'branch', 'tile'), 'dap'), parts along dimension 0
The draws below stay inside these ranges and needn't reach their ends.
There are 2 independent parts, one for each index of `groups`. The reference program is written for one: setup_inputs(seed, part) draws one part's arguments, and reference() takes and returns one part's arrays. A program takes and returns all parts, laid end to end along the dimension named above; an argument that names none is the same for every part. Nothing has to cross between parts.
Inputs may be any that keep to these rules, and one draw needn't show every extreme that they name: `monomer_serials`: starts at 0 and rises by 1 to 3 from each residue to the next. `polymer_labeling`: chains are contiguous runs of 1 to 128 residues, numbered in order.
All inputs are finite; a program needn't handle non-finite values. No bound on the sum of `homolog_valid_flags` or of `duo_valid_flags` on one device may be relied on, other than what follows from the above.
Results may differ from the reference program's by a relative error of at most 0.015.
Values may be sent and summed in bfloat16 or wider, within the bound.
No kernel may reach another device: no remote copies, remote signals or barrier semaphores. Data moves between devices by JAX's collectives and lax.ppermute only.
A program may use at most 128 MiB of HBM per device.

```python
import math
import jax
import jax.numpy as jnp
import numpy as np
from jax import lax

ALIGN_FEATURES = 256
DUAL_DIM = 128
FOCUS_GROUPS = 8
GROUP_CHANNEL = 32
TENSORED_FEATS = 32
TRIAD_DIM = 128
REL_BINS = 66
CUT_AMINO_SITES = 256
ALIGN_STRANDS = 32


def draw_homolog_hidden(key, part):
    seed_stochastic_token = jax.random.normal(key, (ALIGN_STRANDS, CUT_AMINO_SITES, ALIGN_FEATURES), jnp.float32)
    return jnp.clip(seed_stochastic_token, -6.0, 6.0).astype(jnp.bfloat16)


def draw_qkv_valve_projectors(key, part):
    seed_stochastic_token = jax.random.normal(key, (ALIGN_FEATURES, 4 * ALIGN_FEATURES), jnp.float32) * ALIGN_FEATURES ** (-0.5)
    return seed_stochastic_token.astype(jnp.bfloat16)


def draw_monomer_serials(key, part):
    half_count = CUT_AMINO_SITES // 2
    first_steps = jax.random.randint(key, (half_count,), 1, 4, dtype=jnp.int32)
    last_pair = jnp.arange(half_count, dtype=jnp.int32) == half_count - 1
    first_steps = jnp.where(last_pair, jnp.int32(2), first_steps).astype(jnp.int32)
    step_sizes = jnp.stack([first_steps, 4 - first_steps], axis=1).reshape(CUT_AMINO_SITES).astype(jnp.int32)
    running = jnp.cumsum(step_sizes).astype(jnp.int32)
    return jnp.concatenate([jnp.zeros((1,), jnp.int32), running[:-1]]).astype(jnp.int32)


def plant(array, own_key, low, largest):
    dims = array.shape
    spot = [jax.random.randint(jax.random.fold_in(own_key, axis), (), 0, dims[axis]) for axis in range(len(dims))]
    array = array.at[tuple(spot)].set(low)
    longest = dims.index(max(dims))
    spot[longest] = (spot[longest] + 1) % dims[longest]
    return array.at[tuple(spot)].set(largest)


def steps_of(own_key, extent, split, smallest, top_value):
    def one(dim, parts):
        draws = jax.random.uniform(jax.random.fold_in(jax.random.fold_in(own_key, 6), dim), (parts,), jnp.float32, smallest / len(split), top_value / len(split))
        return jnp.repeat(jnp.exp(draws), extent[dim] // parts).reshape((-1,) + (1,) * (len(extent) - dim - 1))

    loudness = one(*split[0])
    for cut in split[1:]:
        loudness = loudness * one(*cut)
    return loudness


def length_profile(number_of, total, reach, slope):
    weights = [(1 << 20) // math.isqrt(standing ** slope) + 1 for standing in range(2, number_of + 1)]
    surplus, given = total - reach - (number_of - 1), [1] * (number_of - 1)
    while surplus > 0:
        candidates = [i for i in range(number_of - 1) if given[i] < reach]
        mass, budget = sum([weights[i] for i in candidates]), surplus
        for i in candidates:
            more = min(reach - given[i], max(1, budget * weights[i] // mass), surplus)
            given[i] = given[i] + more
            surplus = surplus - more
    return np.array([reach] + given)


def uneven_parts(rng, number_of, total, reach, slope):
    if number_of == 2:
        one = jax.random.randint(rng, (), max(1, total - reach), min(reach, total - 1) + 1)
        return jnp.stack([one, total - one])
    tallies = jnp.asarray(length_profile(number_of, total, reach, slope), jnp.int32)
    couples = (number_of - 1) // 2
    donor, sink = tallies[1:1 + 2 * couples:2], tallies[2:2 + 2 * couples:2]
    slack = jnp.minimum(donor - 1, reach - sink)
    passed = jax.random.randint(jax.random.fold_in(rng, 1), (couples,), 0, 1 << 20) % (slack + 1)
    tallies = tallies.at[1:1 + 2 * couples:2].set(donor - passed).at[2:2 + 2 * couples:2].set(sink + passed)
    return tallies[jax.random.permutation(jax.random.fold_in(rng, 2), number_of)]


def noise(stream_key, dims, scale, limit, cuts=(), kind=jnp.bfloat16):
    entries = jax.random.normal(stream_key, dims, jnp.float32) * scale
    if len(cuts) > 0:
        entries = steps_of(stream_key, dims, cuts, -0.22, 0.18) * entries
    return jnp.clip(entries, min=-limit, max=limit).astype(kind)


def setup_inputs(seed: int = 0, part: int = 0) -> dict:
    keys = jax.random.split(jax.random.key(seed), 21)
    part_splits = jax.random.split(jax.random.fold_in(keys[20], part), 21)
    return {
        "homolog_hidden": draw_homolog_hidden(jax.random.fold_in(jax.random.fold_in(keys[20], part), 71), part),
        "duo_hidden": noise(part_splits[1], (CUT_AMINO_SITES, CUT_AMINO_SITES, DUAL_DIM), 1.0, 6.0, ((0, 4), (1, 4))),
        "homolog_valid_flags": plant((jax.random.randint(part_splits[2], (ALIGN_STRANDS, CUT_AMINO_SITES), 0, 8) < 7).astype(jnp.int32), jax.random.fold_in(part_splits[2], 1), 0, 1),
        "duo_valid_flags": plant((jax.random.randint(part_splits[3], (CUT_AMINO_SITES, CUT_AMINO_SITES), 0, 8) < 7).astype(jnp.int32), jax.random.fold_in(part_splits[3], 1), 0, 1),
        "polymer_labeling": jnp.searchsorted(jnp.cumsum(uneven_parts(part_splits[4], 4, CUT_AMINO_SITES, CUT_AMINO_SITES // 2, 0)), jnp.arange(CUT_AMINO_SITES), side="right").astype(jnp.int32),
        "monomer_serials": draw_monomer_serials(jax.random.fold_in(jax.random.fold_in(keys[20], part), 71), part),
        "separation_bin_vectors": noise(keys[6], (REL_BINS, DUAL_DIM), 0.5, 4.0),
        "duo_logit_rescale": jnp.clip(1.0 + 0.15 * jax.random.normal(keys[7], (DUAL_DIM,), jnp.float32), 0.25, 1.75),
        "duo_logit_projector": noise(keys[8], (DUAL_DIM, FOCUS_GROUPS), DUAL_DIM ** -0.5, 0.5),
        "homolog_heeded_rescale": jnp.clip(1.0 + 0.15 * jax.random.normal(keys[9], (ALIGN_FEATURES,), jnp.float32), 0.25, 1.75),
        "qkv_valve_projectors": draw_qkv_valve_projectors(jax.random.fold_in(keys[20], 71), part),
        "heeded_exit_projector": noise(keys[11], (ALIGN_FEATURES, ALIGN_FEATURES), ALIGN_FEATURES ** -0.5, 0.375),
        "dyadic_rescale": jnp.clip(1.0 + 0.15 * jax.random.normal(keys[12], (ALIGN_FEATURES,), jnp.float32), 0.25, 1.75),
        "dyadic_factor_projector": noise(keys[13], (ALIGN_FEATURES, 2 * TENSORED_FEATS), ALIGN_FEATURES ** -0.5, 0.375),
        "dyadic_exit_projector": noise(keys[14], (TENSORED_FEATS * TENSORED_FEATS, DUAL_DIM), (TENSORED_FEATS * TENSORED_FEATS // 64) ** -0.5, 1.5),
        "triad_entry_rescales": jnp.clip(1.0 + 0.15 * jax.random.normal(keys[15], (2, DUAL_DIM), jnp.float32), 0.25, 1.75),
        "triad_entry_projectors": noise(keys[16], (2, DUAL_DIM, 4 * TRIAD_DIM), DUAL_DIM ** -0.5, 0.5),
        "triad_valve_projectors": noise(keys[17], (2, DUAL_DIM, DUAL_DIM), DUAL_DIM ** -0.5, 0.5),
        "triad_exit_rescales": jnp.clip(1.0 + 0.15 * jax.random.normal(keys[18], (2, TRIAD_DIM), jnp.float32), 0.25, 1.75),
        "triad_exit_projectors": noise(keys[19], (2, TRIAD_DIM, DUAL_DIM), TRIAD_DIM ** -0.5, 0.5),
    }


norm_eps = 1e-05
mask_big = 1000000000.0
count_eps = 0.001

def quantized_entries(values):
    return lax.optimization_barrier(values.astype(jnp.bfloat16))

def standardize_features(values, norm_gain):
    values = values.astype(jnp.float32)
    mean_val = lax.optimization_barrier(jnp.mean(values, axis=-1, keepdims=True))
    centred = values - mean_val
    spread = lax.optimization_barrier(jnp.mean(centred * centred, axis=-1, keepdims=True))
    return centred * lax.rsqrt(spread + norm_eps) * norm_gain.astype(jnp.float32)

def unrolled_tensored_term(values, weight):
    lead_shape = values.shape[:-1]
    flat_out = jnp.dot(values.reshape(-1, values.shape[-1]), weight, preferred_element_type=jnp.float32)
    return flat_out.reshape(lead_shape + (weight.shape[1],))

def threeway_update(duo_hidden_values, duo_valid_flags, norm_gain, w_in, w_gate, out_gain, w_out, incoming):
    tri_normed = quantized_entries(standardize_features(duo_hidden_values, norm_gain))
    mapped_contents = unrolled_tensored_term(tri_normed, w_in)
    width_tri = w_in.shape[1] // 4
    mask_as_float = duo_valid_flags.astype(jnp.float32)[..., None]
    left_fac = quantized_entries(jax.nn.sigmoid(mapped_contents[..., width_tri:2 * width_tri]) * mapped_contents[..., :width_tri] * mask_as_float)
    right_fac = quantized_entries(jax.nn.sigmoid(mapped_contents[..., 3 * width_tri:]) * mapped_contents[..., 2 * width_tri:3 * width_tri] * mask_as_float)
    if incoming:
        einsum_form = 'kic,kjc->ijc'
    else:
        einsum_form = 'ikc,jkc->ijc'
    product = quantized_entries(jnp.einsum(einsum_form, left_fac.astype(jnp.float32), right_fac.astype(jnp.float32), precision=lax.Precision.HIGHEST))
    product_normed = quantized_entries(standardize_features(product, out_gain))
    sigmoid_switches = jax.nn.sigmoid(unrolled_tensored_term(tri_normed, w_gate))
    return duo_hidden_values + sigmoid_switches * unrolled_tensored_term(product_normed, w_out)

def reference(homolog_hidden, duo_hidden, homolog_valid_flags, duo_valid_flags, polymer_labeling, monomer_serials, separation_bin_vectors, duo_logit_rescale, duo_logit_projector, homolog_heeded_rescale, qkv_valve_projectors, heeded_exit_projector, dyadic_rescale, dyadic_factor_projector, dyadic_exit_projector, triad_entry_rescales, triad_entry_projectors, triad_valve_projectors, triad_exit_rescales, triad_exit_projectors):
    rel_reach = (REL_BINS - 2) // 2
    offset = jnp.clip(monomer_serials[:, None] - monomer_serials[None, :], -rel_reach, rel_reach) + rel_reach
    rel_bins = jnp.where(polymer_labeling[:, None] == polymer_labeling[None, :], offset, REL_BINS - 1).astype(jnp.int32)
    duo_hidden_values = duo_hidden.astype(jnp.float32) + separation_bin_vectors.astype(jnp.float32)[rel_bins]
    pair_normed = quantized_entries(standardize_features(duo_hidden_values, duo_logit_rescale))
    pair_bias = jnp.transpose(quantized_entries(unrolled_tensored_term(pair_normed, duo_logit_projector)), (2, 0, 1)).astype(jnp.float32)
    lineup_standardized = quantized_entries(standardize_features(homolog_hidden, homolog_heeded_rescale))
    mapped_contents = unrolled_tensored_term(lineup_standardized, qkv_valve_projectors)
    asking_array = quantized_entries(mapped_contents[..., :ALIGN_FEATURES] * GROUP_CHANNEL ** (-0.5))
    lookup_strand_lines = quantized_entries(mapped_contents[..., ALIGN_FEATURES:2 * ALIGN_FEATURES])
    content_strand_lines = quantized_entries(mapped_contents[..., 2 * ALIGN_FEATURES:3 * ALIGN_FEATURES])
    sigmoid_switches = jax.nn.sigmoid(mapped_contents[..., 3 * ALIGN_FEATURES:])

    def attend_single_row(row_args):
        query_row, key_row, value_row, mask_row = row_args
        query_heads = query_row.astype(jnp.float32).reshape(CUT_AMINO_SITES, FOCUS_GROUPS, GROUP_CHANNEL)
        key_per_head = key_row.astype(jnp.float32).reshape(CUT_AMINO_SITES, FOCUS_GROUPS, GROUP_CHANNEL)
        value_per_head = value_row.astype(jnp.float32).reshape(CUT_AMINO_SITES, FOCUS_GROUPS, GROUP_CHANNEL)
        scores = jnp.einsum('ihd,jhd->hij', query_heads, key_per_head, precision=lax.Precision.HIGHEST)
        scores = scores + pair_bias + ((mask_row.astype(jnp.float32) - 1.0) * mask_big)[None, None, :]
        row_max = lax.optimization_barrier(jnp.max(scores, axis=-1, keepdims=True))
        weights = jnp.exp(scores - row_max)
        row_sum = lax.optimization_barrier(jnp.sum(weights, axis=-1))
        weights_bf = quantized_entries(weights).astype(jnp.float32)
        focused_readout = jnp.einsum('hij,jhd->ihd', weights_bf, value_per_head, precision=lax.Precision.HIGHEST)
        focused_readout = focused_readout / jnp.transpose(row_sum)[:, :, None]
        return focused_readout.reshape(CUT_AMINO_SITES, ALIGN_FEATURES)
    focused_readout = lax.map(attend_single_row, (asking_array, lookup_strand_lines, content_strand_lines, homolog_valid_flags))
    merged_focus_groups = quantized_entries(sigmoid_switches * focused_readout)
    lineup_updated_state = (homolog_hidden.astype(jnp.float32) + unrolled_tensored_term(merged_focus_groups, heeded_exit_projector)).astype(jnp.bfloat16)
    outer_product_normalized = quantized_entries(standardize_features(lineup_updated_state, dyadic_rescale))
    mask_as_float = homolog_valid_flags.astype(jnp.float32)
    factors = unrolled_tensored_term(outer_product_normalized, dyadic_factor_projector) * mask_as_float[..., None]
    left_fac = quantized_entries(factors[..., :TENSORED_FEATS]).astype(jnp.float32)
    right_fac = quantized_entries(factors[..., TENSORED_FEATS:]).astype(jnp.float32)
    counts = jnp.einsum('si,sj->ij', mask_as_float, mask_as_float, precision=lax.Precision.HIGHEST)
    row_block = 16

    def outer_rows(first_row):
        left_factor_rows = lax.dynamic_slice_in_dim(left_fac, first_row, row_block, 1)
        outer_prod = quantized_entries(jnp.einsum('sic,sjd->ijcd', left_factor_rows, right_fac, precision=lax.Precision.HIGHEST)).astype(jnp.float32)
        outer_prod = outer_prod.reshape(row_block, CUT_AMINO_SITES, TENSORED_FEATS * TENSORED_FEATS)
        return jnp.einsum('ijk,kz->ijz', outer_prod, dyadic_exit_projector.astype(jnp.float32), precision=lax.Precision.HIGHEST)
    first_rows = jnp.arange(CUT_AMINO_SITES // row_block, dtype=jnp.int32) * row_block
    update = lax.map(outer_rows, first_rows).reshape(CUT_AMINO_SITES, CUT_AMINO_SITES, DUAL_DIM)
    duo_hidden_values = duo_hidden_values + update / (count_eps + counts)[..., None]
    for threefold_module in range(2):
        duo_hidden_values = threeway_update(duo_hidden_values, duo_valid_flags, triad_entry_rescales[threefold_module], triad_entry_projectors[threefold_module], triad_valve_projectors[threefold_module], triad_exit_rescales[threefold_module], triad_exit_projectors[threefold_module], threefold_module == 1)
    return (lineup_updated_state, duo_hidden_values.astype(jnp.bfloat16))
```

```python
import functools

import jax
import jax.numpy as jnp
from jax import lax
from jax.experimental import pallas as pl
from jax.experimental.pallas import tpu as pltpu
from jax.sharding import PartitionSpec as P

REL_BINS = 66
LANES = 128
HALF = 64
VMEM_BYTES = 56 * 1024 * 1024
WHOLE = ("branch", "dap", "tile")


norm_eps = 1e-05
mask_big = 1000000000.0
count_eps = 0.001


def standardize_features(values, norm_gain, norm_axis):
    values = values.astype(jnp.float32)
    mean_val = jnp.mean(values, axis=norm_axis, keepdims=True)
    centred = values - mean_val
    spread = jnp.mean(centred * centred, axis=norm_axis, keepdims=True)
    return centred * lax.rsqrt(spread + norm_eps) * norm_gain


def threeway_update(
    duo_hidden_values, duo_valid_flags, norm_gain, w_in, w_gate, out_gain, w_out, incoming
):
    width_tri = w_in.shape[1] // 4
    tri_normed = standardize_features(duo_hidden_values, norm_gain, 2).astype(jnp.bfloat16)
    mapped_contents = jnp.einsum(
        "ijc,cd->idj", tri_normed, w_in, preferred_element_type=jnp.float32
    )
    mask_as_float = duo_valid_flags.astype(jnp.float32)[:, None, :]
    left_fac = (
        jax.nn.sigmoid(mapped_contents[:, width_tri : 2 * width_tri])
        * mapped_contents[:, :width_tri]
        * mask_as_float
    ).astype(jnp.bfloat16)
    right_fac = (
        jax.nn.sigmoid(mapped_contents[:, 3 * width_tri :])
        * mapped_contents[:, 2 * width_tri : 3 * width_tri]
        * mask_as_float
    ).astype(jnp.bfloat16)
    sigmoid_switches = jax.nn.sigmoid(
        jnp.einsum("ijc,cd->ijd", tri_normed, w_gate, preferred_element_type=jnp.float32)
    )
    left_split, right_split = (
        lax.all_to_all(left_fac, "dap", split_axis=1, concat_axis=2, tiled=True),
        lax.all_to_all(right_fac, "dap", split_axis=1, concat_axis=2, tiled=True),
    )
    if not incoming:
        product = jnp.einsum(
            "ick,jck->icj",
            left_split,
            lax.all_gather(right_split, ("branch", "tile"), axis=0, tiled=True),
            preferred_element_type=jnp.float32,
        )
    else:
        product = lax.psum_scatter(
            jnp.einsum(
                "kci,kcj->icj", left_split, right_split, preferred_element_type=jnp.float32
            ).astype(jnp.bfloat16),
            ("branch", "tile"),
            scatter_dimension=0,
            tiled=True,
        ).astype(jnp.float32)
    merged = lax.all_to_all(
        product.astype(jnp.bfloat16), "dap", split_axis=2, concat_axis=1, tiled=True
    )
    product_normed = standardize_features(merged, out_gain[:, None], 1).astype(jnp.bfloat16)
    update = jnp.einsum("icj,cz->ijz", product_normed, w_out, preferred_element_type=jnp.float32)
    return duo_hidden_values + sigmoid_switches * update


def body(
    homolog_hidden,
    duo_hidden,
    homolog_valid_flags,
    duo_valid_flags,
    polymer_labeling,
    monomer_serials,
    separation_bin_vectors,
    duo_logit_rescale,
    duo_logit_projector,
    homolog_heeded_rescale,
    qkv_valve_projectors,
    heeded_exit_projector,
    dyadic_rescale,
    dyadic_factor_projector,
    dyadic_exit_projector,
    triad_entry_rescales,
    triad_entry_projectors,
    triad_valve_projectors,
    triad_exit_rescales,
    triad_exit_projectors,
):
    lines_each_shard, sites_each_shard, lineup_feature_extent = homolog_hidden.shape
    columns_per_device = duo_hidden.shape[1]
    number_of_heads = duo_logit_projector.shape[1]
    head_channels = lineup_feature_extent // number_of_heads
    outer_channels = dyadic_factor_projector.shape[1] // 2
    row_start = lax.axis_index(("branch", "tile")) * sites_each_shard
    col_start = lax.axis_index("dap") * columns_per_device
    rel_reach = (REL_BINS - 2) // 2
    res_rows = lax.dynamic_slice_in_dim(monomer_serials, row_start, sites_each_shard)
    res_cols = lax.dynamic_slice_in_dim(monomer_serials, col_start, columns_per_device)
    chain_rows = lax.dynamic_slice_in_dim(polymer_labeling, row_start, sites_each_shard)
    chain_cols = lax.dynamic_slice_in_dim(polymer_labeling, col_start, columns_per_device)
    offset = jnp.clip(res_rows[:, None] - res_cols[None, :], -rel_reach, rel_reach) + rel_reach
    rel_bins = jnp.where(chain_rows[:, None] == chain_cols[None, :], offset, REL_BINS - 1)
    one_hot = (rel_bins[:, :, None] == jnp.arange(REL_BINS, dtype=jnp.int32)[None, None, :]).astype(
        jnp.bfloat16
    )
    duo_hidden_values = duo_hidden.astype(jnp.float32) + jnp.einsum(
        "ijb,bc->ijc", one_hot, separation_bin_vectors, preferred_element_type=jnp.float32
    )
    pair_normed = standardize_features(duo_hidden_values, duo_logit_rescale, 2).astype(jnp.bfloat16)
    local_bias = jnp.einsum(
        "ijc,ch->hij", pair_normed, duo_logit_projector, preferred_element_type=jnp.float32
    ).astype(jnp.bfloat16)
    row_bias = lax.all_gather(local_bias, "dap", axis=2, tiled=True)
    lineup_standardized = standardize_features(homolog_hidden, homolog_heeded_rescale, 2).astype(
        jnp.bfloat16
    )
    mapped_contents = jnp.einsum(
        "ezp,pb->ezb", lineup_standardized, qkv_valve_projectors, preferred_element_type=jnp.float32
    )
    asking_array = (mapped_contents[..., :lineup_feature_extent] * head_channels ** (-0.5)).astype(
        jnp.bfloat16
    )
    asking_array = asking_array.reshape(
        lines_each_shard, sites_each_shard, number_of_heads, head_channels
    )
    key_value_pairs = mapped_contents[
        ..., lineup_feature_extent : 3 * lineup_feature_extent
    ].astype(jnp.bfloat16)
    sigmoid_switches = jax.nn.sigmoid(mapped_contents[..., 3 * lineup_feature_extent :])
    mask_as_float = homolog_valid_flags.astype(jnp.bfloat16)
    run_max = jnp.full((lines_each_shard, number_of_heads, sites_each_shard), -jnp.inf, jnp.float32)
    run_sum = jnp.zeros((lines_each_shard, number_of_heads, sites_each_shard), jnp.float32)
    run_acc = jnp.zeros(
        (lines_each_shard, number_of_heads, sites_each_shard, head_channels), jnp.float32
    )
    key_value_slice = lax.all_gather(key_value_pairs, ("branch", "tile"), axis=1, tiled=True)
    mask_piece = lax.all_gather(mask_as_float, ("branch", "tile"), axis=1, tiled=True)
    slice_length = key_value_slice.shape[1]
    key_per_head = key_value_slice[..., :lineup_feature_extent].reshape(
        lines_each_shard, slice_length, number_of_heads, head_channels
    )
    value_per_head = key_value_slice[..., lineup_feature_extent:].reshape(
        lines_each_shard, slice_length, number_of_heads, head_channels
    )
    key_bias = row_bias.astype(jnp.float32)
    scores = jnp.einsum(
        "sihd,sjhd->shij", asking_array, key_per_head, preferred_element_type=jnp.float32
    )
    scores = (
        scores
        + key_bias[None]
        + ((mask_piece.astype(jnp.float32) - 1.0) * mask_big)[:, None, None, :]
    )
    new_max = jnp.max(scores, axis=-1)
    old_scale = jnp.exp(run_max - new_max)
    weights = jnp.exp(scores - new_max[..., None])
    run_sum = run_sum * old_scale + jnp.sum(weights, axis=-1)
    run_acc = run_acc * old_scale[..., None] + jnp.einsum(
        "shij,sjhd->shid",
        weights.astype(jnp.bfloat16),
        value_per_head,
        preferred_element_type=jnp.float32,
    )
    run_max, run_sum, run_acc = (new_max, run_sum, run_acc)
    focused_readout = run_acc / run_sum[..., None]
    focused_readout = jnp.transpose(focused_readout, (0, 2, 1, 3)).reshape(
        lines_each_shard, sites_each_shard, lineup_feature_extent
    )
    merged_focus_groups = (sigmoid_switches * focused_readout).astype(jnp.bfloat16)
    lineup_updated_state = (
        homolog_hidden.astype(jnp.float32)
        + jnp.einsum(
            "ezp,pb->ezb",
            merged_focus_groups,
            heeded_exit_projector,
            preferred_element_type=jnp.float32,
        )
    ).astype(jnp.bfloat16)
    outer_product_normalized = standardize_features(lineup_updated_state, dyadic_rescale, 2).astype(
        jnp.bfloat16
    )
    factors = (
        jnp.einsum(
            "ezp,pb->ezb",
            outer_product_normalized,
            dyadic_factor_projector,
            preferred_element_type=jnp.float32,
        )
        * homolog_valid_flags.astype(jnp.float32)[..., None]
    )
    left_flat = (
        factors[..., :outer_channels]
        .astype(jnp.bfloat16)
        .reshape(lines_each_shard, sites_each_shard * outer_channels)
    )
    right_flat = (
        factors[..., outer_channels:]
        .astype(jnp.bfloat16)
        .reshape(lines_each_shard, sites_each_shard * outer_channels)
    )
    right_all, mask_all = (
        lax.all_gather(right_flat, ("branch", "tile"), axis=1, tiled=True),
        lax.all_gather(mask_as_float, ("branch", "tile"), axis=1, tiled=True),
    )
    total_res = mask_all.shape[1]
    right_all = right_all.reshape(lines_each_shard, total_res, outer_channels)
    right_factor_rows, mask_right = (
        lax.all_to_all(right_all, "dap", split_axis=1, concat_axis=0, tiled=True),
        lax.all_to_all(mask_all, "dap", split_axis=1, concat_axis=0, tiled=True),
    )
    left_factor_rows, mask_rows = (
        lax.all_gather(left_flat, "dap", axis=0, tiled=True),
        lax.all_gather(mask_as_float, "dap", axis=0, tiled=True),
    )
    alignment_rows = left_factor_rows.shape[0]
    left_factor_rows = left_factor_rows.reshape(alignment_rows, sites_each_shard, outer_channels)
    counts = jnp.einsum("si,sj->ij", mask_rows, mask_right, preferred_element_type=jnp.float32)
    outer_prod = jnp.einsum(
        "sic,sjd->ijcd", left_factor_rows, right_factor_rows, preferred_element_type=jnp.float32
    ).astype(jnp.bfloat16)
    outer_prod = outer_prod.reshape(
        sites_each_shard, columns_per_device, outer_channels * outer_channels
    )
    update = jnp.einsum(
        "ijk,kz->ijz", outer_prod, dyadic_exit_projector, preferred_element_type=jnp.float32
    )
    duo_hidden_values = duo_hidden_values + update / (count_eps + counts)[..., None]
    for threefold_module in range(2):
        duo_hidden_values = threeway_update(
            duo_hidden_values,
            duo_valid_flags,
            triad_entry_rescales[threefold_module],
            triad_entry_projectors[threefold_module],
            triad_valve_projectors[threefold_module],
            triad_exit_rescales[threefold_module],
            triad_exit_projectors[threefold_module],
            threefold_module == 1,
        )
    return (lineup_updated_state, duo_hidden_values.astype(jnp.bfloat16))


def standardize_sublanes(values, gain):
    mean_val = jnp.mean(values, axis=0, keepdims=True)
    centred = values - mean_val
    spread = jnp.mean(centred * centred, axis=0, keepdims=True)
    return (centred * lax.rsqrt(spread + norm_eps) * gain).astype(jnp.bfloat16)


def standardize_lanes(values, gain):
    mean_val = jnp.mean(values, axis=-1, keepdims=True)
    centred = values - mean_val
    spread = jnp.mean(centred * centred, axis=-1, keepdims=True)
    return (centred * lax.rsqrt(spread + norm_eps) * gain).astype(jnp.bfloat16)


def matmul(a, b, dims=((1,), (0,))):
    return lax.dot_general(a, b, (dims, ((), ())), preferred_element_type=jnp.float32)


def swap_halves(first, second):
    low = lax.broadcasted_iota(jnp.int32, first.shape, first.ndim - 1) < HALF
    turned_first = pltpu.roll(first, HALF, first.ndim - 1)
    turned_second = pltpu.roll(second, HALF, second.ndim - 1)
    return jnp.where(low, first, turned_second), jnp.where(low, turned_first, second)


def column_of(row):
    return jnp.broadcast_to(row, (row.shape[1], row.shape[1])).T


def opening_kernel(duo, bins, table_t, gain, projector_t, state, bias):
    gain_col = column_of(gain[...])
    levels = lax.broadcasted_iota(jnp.int32, (LANES, LANES), 0)
    pairs = state.shape[0]

    def step(p, carry):
        block = jnp.concatenate([duo[p], duo[p + pairs]], axis=0)
        one_hot = (levels == bins[pl.ds(p, 1), :]).astype(jnp.bfloat16)
        value = block.astype(jnp.float32).T + matmul(table_t[...], one_hot)
        state[p] = value
        normed = standardize_sublanes(value, gain_col)
        bias[p] = matmul(projector_t[...], normed).astype(jnp.bfloat16)
        return carry

    lax.fori_loop(0, pairs, step, 0, unroll=2)


def attention_kernel(
    place, own, near, cross, far, flags_own, flags_near, flags_cross, flags_far,
    bias_0, bias_1, bias_2, bias_3, gain, projectors, exit_projector, outer_gain, factor_projector,
    updated, factors,
    bias_in, bias_all, flag_all, keys, vals, query, gate, mixed,
):
    row, col = place[0], place[1]
    lines, sites, feats = own.shape
    heads = bias_0.shape[1]
    width = feats // heads
    pairs = bias_0.shape[0]
    for k, piece in enumerate((bias_0, bias_1, bias_2, bias_3)):
        bias_in[col ^ k] = piece[...].astype(jnp.float32).reshape(pairs * heads, LANES)
    for k, piece in enumerate((flags_own, flags_near, flags_cross, flags_far)):
        flag_all[row ^ k] = piece[...].astype(jnp.float32)
    for head in range(heads):
        for pair in range(2):
            first = bias_in[2 * pair, pl.ds(head, pairs, stride=heads), :]
            second = bias_in[2 * pair + 1, pl.ds(head, pairs, stride=heads), :]
            upper, lower = swap_halves(first, second)
            bias_all[head * sites : head * sites + pairs, pair * LANES : (pair + 1) * LANES] = upper
            bias_all[head * sites + pairs : (head + 1) * sites, pair * LANES : (pair + 1) * LANES] = lower
    for k, piece in enumerate((own, near, cross, far)):
        normed = standardize_lanes(
            piece[...].astype(jnp.float32).reshape(lines * sites, feats), gain[...]
        )
        both = matmul(normed, projectors[:, feats : 3 * feats]).astype(jnp.bfloat16)
        keys[row ^ k] = both[:, :feats].reshape(lines, sites, feats)
        vals[row ^ k] = both[:, feats:].reshape(lines, sites, feats)
        if k == 0:
            query[...] = (
                (matmul(normed, projectors[:, :feats]) * width ** (-0.5))
                .astype(jnp.bfloat16)
                .reshape(lines, sites, feats)
            )
            gate[...] = jax.nn.sigmoid(matmul(normed, projectors[:, 3 * feats :])).reshape(
                lines, sites, feats
            )
    lane_head = lax.broadcasted_iota(jnp.int32, (sites, feats), 1) // width

    def step(s, carry):
        q = query[s].astype(jnp.float32)
        q_all = jnp.concatenate(
            [jnp.where(lane_head == h, q, 0.0) for h in range(heads)], axis=0
        ).astype(jnp.bfloat16)
        k_all = jnp.concatenate([keys[b, s] for b in range(4)], axis=0)
        v_all = jnp.concatenate([vals[b, s] for b in range(4)], axis=0)
        flag_rows = [flag_all[b, pl.ds(s, 1), :] for b in range(4)]
        flag_row = jnp.concatenate(
            [
                swap_halves(flag_rows[0], flag_rows[1])[0],
                swap_halves(flag_rows[2], flag_rows[3])[0],
            ],
            axis=1,
        )
        scores = matmul(q_all, k_all, ((1,), (1,))) + bias_all[...]
        scores = scores + (flag_row - 1.0) * mask_big
        weights = jnp.exp(scores - jnp.max(scores, axis=-1, keepdims=True))
        total = jnp.sum(weights, axis=-1, keepdims=True)
        read = matmul(weights.astype(jnp.bfloat16), v_all) / total
        picked = jnp.zeros((sites, feats), jnp.float32)
        for h in range(heads):
            picked = jnp.where(lane_head == h, read[h * sites : (h + 1) * sites], picked)
        mixed[s] = (gate[s] * picked).astype(jnp.bfloat16)
        return carry

    lax.fori_loop(0, lines, step, 0)
    new = own[...].astype(jnp.float32).reshape(lines * sites, feats) + matmul(
        mixed[...].reshape(lines * sites, feats), exit_projector[...]
    )
    new = new.astype(jnp.bfloat16)
    updated[...] = new.reshape(lines, sites, feats)
    normed = standardize_lanes(new.astype(jnp.float32), outer_gain[...])
    factors[...] = matmul(normed, factor_projector[...]).reshape(lines, sites, -1)


def send_factors(value, p, entry_t, gain_col, mask, parcel):
    normed = standardize_sublanes(value, gain_col)
    mapped = matmul(entry_t[...], normed)
    width = value.shape[0]
    flag = mask
    left = jax.nn.sigmoid(mapped[width : 2 * width]) * mapped[:width] * flag
    right = jax.nn.sigmoid(mapped[3 * width :]) * mapped[2 * width : 3 * width] * flag
    parts = parcel.shape[0]
    both = jnp.concatenate(
        [left.reshape(parts, -1, LANES), right.reshape(parts, -1, LANES)], axis=1
    )
    parcel[:, p] = both.astype(jnp.bfloat16)


def outer_kernel(
    place, left_0, left_1, left_2, left_3, right_0, right_1, right_2, right_3,
    state, outer_t, mask, gain, entry_t,
    new_state, parcel,
    left_all, right_all, left_t, right_wide, outer, scale,
):
    row, col = place[0], place[1]
    lines = left_0.shape[0]
    pairs, width = state.shape[0], state.shape[1]
    for k, piece in enumerate((left_0, left_1, left_2, left_3)):
        left_all[col ^ k] = piece[...].astype(jnp.float32)
    for k, piece in enumerate((right_0, right_1, right_2, right_3)):
        right_all[row ^ k] = piece[...].astype(jnp.float32)
    total = left_all.shape[0] * lines
    span = left_all.shape[2] - LANES
    left = left_all[...].reshape(total, span + LANES)
    right = right_all[...].reshape(total, span + LANES)
    stacked = jnp.concatenate([left[:, : span // 2], left[:, span // 2 : span]], axis=0)
    left_t[...] = stacked.T.astype(jnp.bfloat16)
    feats = span // HALF // 2
    tiles = span // LANES
    low = lax.broadcasted_iota(jnp.int32, (total, LANES), 1) < HALF
    for t in range(tiles):
        piece = right[:, t * LANES : (t + 1) * LANES]
        turned = pltpu.roll(piece, HALF, 1)
        first = jnp.concatenate([jnp.where(low, piece, 0.0), jnp.where(low, 0.0, turned)], axis=0)
        second = jnp.concatenate([jnp.where(low, turned, 0.0), jnp.where(low, 0.0, piece)], axis=0)
        right_wide[t] = jnp.concatenate([first, second], axis=1).astype(jnp.bfloat16)
    flags_left = left[:, span:]
    flags_left = jnp.concatenate([flags_left, pltpu.roll(flags_left, LANES - HALF // 2, 1)], axis=0)
    flags_left = flags_left.T[:pairs].astype(jnp.bfloat16)
    flags_right = right[:, span:]
    flags_right = jnp.concatenate(
        [jnp.where(low, flags_right, 0.0), jnp.where(low, 0.0, pltpu.roll(flags_right, HALF, 1))],
        axis=0,
    ).astype(jnp.bfloat16)
    scale[...] = 1.0 / (count_eps + matmul(flags_left, flags_right))
    chans = left_t.shape[0] // pairs

    def expand(t, carry):
        tile = matmul(left_t[...], right_wide[t])
        for half in range(2):
            outer[:, 2 * t + half] = (
                tile[:, half * LANES : (half + 1) * LANES]
                .reshape(pairs, chans, LANES)
                .astype(jnp.bfloat16)
            )
        return carry

    lax.fori_loop(0, tiles, expand, 0)
    gain_col = column_of(gain[...])

    def step(q, carry):
        p = 2 * q
        flat = jnp.concatenate(
            [outer[p].reshape(-1, LANES), outer[p + 1].reshape(-1, LANES)], axis=1
        )
        update = matmul(outer_t[...], flat)
        for half in range(2):
            value = state[p + half] + update[:, half * LANES : (half + 1) * LANES] * scale[
                pl.ds(p + half, 1), :
            ]
            new_state[p + half] = value
            send_factors(value, p + half, entry_t, gain_col, mask[pl.ds(p + half, 1), :], parcel)
        return carry

    lax.fori_loop(0, pairs // 2, step, 0)


def product_kernel(incoming, shape, parcel, result, buffer, left, right, wide):
    branches, columns, tiles = shape
    pairs, both = parcel.shape[1], parcel.shape[2]
    chans = both // 2
    sites = 2 * pairs
    for b in range(branches):
        for t in range(tiles):
            row = b * tiles + t
            for pair in range(columns // 2):
                for e in range(2):
                    src = (b * columns + 2 * pair + e) * tiles + t
                    buffer[e] = parcel[src].astype(jnp.float32).reshape(pairs * both, LANES)
                for c in range(both):
                    upper, lower = swap_halves(
                        buffer[0, pl.ds(c, pairs, stride=both), :],
                        buffer[1, pl.ds(c, pairs, stride=both), :],
                    )
                    target = left if c < chans else right
                    lanes = slice(pair * LANES, (pair + 1) * LANES)
                    target[c % chans, row * sites : row * sites + pairs, lanes] = upper.astype(
                        jnp.bfloat16
                    )
                    target[c % chans, row * sites + pairs : (row + 1) * sites, lanes] = lower.astype(
                        jnp.bfloat16
                    )
    dims = ((0,), (0,)) if incoming else ((1,), (1,))
    for c in range(chans):
        value = matmul(left[c], right[c], dims)
        for b in range(branches):
            for t in range(tiles):
                row = b * tiles + t
                for pair in range(columns // 2):
                    lanes = slice(pair * LANES, (pair + 1) * LANES)
                    halves = swap_halves(
                        value[row * sites : row * sites + pairs, lanes],
                        value[row * sites + pairs : (row + 1) * sites, lanes],
                    )
                    for e in range(2):
                        dst = (b * columns + 2 * pair + e) * tiles + t
                        wide[dst, pl.ds(c, pairs, stride=chans), :] = halves[e]
    result[...] = wide[...].reshape(result.shape).astype(jnp.bfloat16)


def merged_update(p, parcel, state, gain_in, valve_t, gain_out, exit_t):
    value = state[p]
    normed = standardize_sublanes(value, gain_in)
    switch = jax.nn.sigmoid(matmul(valve_t[...], normed))
    product = parcel[:, p].astype(jnp.float32).reshape(value.shape)
    update = matmul(exit_t[...], standardize_sublanes(product, gain_out))
    return value + switch * update


def between_kernel(
    parcel, state, gain_in, valve_t, gain_out, exit_t, mask, gain, entry_t, new_state, new_parcel
):
    gains = [column_of(g[...]) for g in (gain_in, gain_out, gain)]

    def step(p, carry):
        value = merged_update(p, parcel, state, gains[0], valve_t, gains[1], exit_t)
        new_state[p] = value
        send_factors(value, p, entry_t, gains[2], mask[pl.ds(p, 1), :], new_parcel)
        return carry

    lax.fori_loop(0, state.shape[0], step, 0, unroll=2)


def closing_kernel(parcel, state, gain_in, valve_t, gain_out, exit_t, out):
    gains = [column_of(g[...]) for g in (gain_in, gain_out)]
    pairs = state.shape[0]
    cols = out.shape[1]

    def step(p, carry):
        value = merged_update(p, parcel, state, gains[0], valve_t, gains[1], exit_t)
        turned = value.T.astype(jnp.bfloat16)
        out[p] = turned[:cols]
        out[p + pairs] = turned[cols:]
        return carry

    lax.fori_loop(0, pairs, step, 0, unroll=2)


def call(kernel, name, out_shape, args, scratch=(), scalars=0):
    spec = pl.BlockSpec(memory_space=pltpu.VMEM)
    return pl.pallas_call(
        kernel,
        name=name,
        out_shape=out_shape,
        in_specs=[pl.BlockSpec(memory_space=pltpu.SMEM)] * scalars + [spec] * (len(args) - scalars),
        out_specs=jax.tree.map(lambda _: spec, out_shape),
        scratch_shapes=scratch,
        compiler_params=pltpu.CompilerParams(vmem_limit_bytes=VMEM_BYTES),
    )(*args)


def fast_body(
    homolog_hidden,
    duo_hidden,
    homolog_valid_flags,
    duo_valid_flags,
    polymer_labeling,
    monomer_serials,
    separation_bin_vectors,
    duo_logit_rescale,
    duo_logit_projector,
    homolog_heeded_rescale,
    qkv_valve_projectors,
    heeded_exit_projector,
    dyadic_rescale,
    dyadic_factor_projector,
    dyadic_exit_projector,
    triad_entry_rescales,
    triad_entry_projectors,
    triad_valve_projectors,
    triad_exit_rescales,
    triad_exit_projectors,
):
    f32, bf16 = jnp.float32, jnp.bfloat16
    struct = jax.ShapeDtypeStruct
    lines, sites, feats = homolog_hidden.shape
    columns, width = duo_hidden.shape[1:]
    heads = duo_logit_projector.shape[1]
    outer_channels = dyadic_factor_projector.shape[1] // 2
    shape = tuple(lax.axis_size(axis) for axis in WHOLE)
    parts = shape[0] * shape[1] * shape[2]
    pairs = sites // 2
    chans = width // parts
    row = lax.axis_index(("branch", "tile"))
    col = lax.axis_index("dap")
    place = jnp.stack([row, col]).astype(jnp.int32)
    flip = [(0, 1), (1, 0)]

    def over(values, axis):
        return lax.ppermute(values, axis, flip)

    def shifted(values, k):
        return lax.ppermute(values, "dap", [(i, i ^ k) for i in range(shape[1])])

    near = over(homolog_hidden, "tile")
    flags = jnp.pad(homolog_valid_flags.astype(bf16), ((0, 0), (0, LANES - sites)))
    flags_near = over(flags, "tile")
    cross = over(homolog_hidden, "branch")
    flags_cross = over(flags, "branch")
    far = over(near, "branch")
    flags_far = over(flags_near, "branch")

    rel_reach = (REL_BINS - 2) // 2
    res_rows = lax.dynamic_slice_in_dim(monomer_serials, row * sites, sites)
    res_cols = lax.dynamic_slice_in_dim(monomer_serials, col * columns, columns)
    chain_rows = lax.dynamic_slice_in_dim(polymer_labeling, row * sites, sites)
    chain_cols = lax.dynamic_slice_in_dim(polymer_labeling, col * columns, columns)
    offset = jnp.clip(res_rows[:, None] - res_cols[None, :], -rel_reach, rel_reach) + rel_reach
    bins = jnp.where(chain_rows[:, None] == chain_cols[None, :], offset, REL_BINS - 1)
    bins = jnp.concatenate([bins[:pairs], bins[pairs:]], axis=1)
    mask = duo_valid_flags.astype(f32)
    mask = jnp.concatenate([mask[:pairs], mask[pairs:]], axis=1)
    table_t = jnp.pad(separation_bin_vectors, ((0, LANES - REL_BINS), (0, 0))).T

    state, bias = call(
        opening_kernel,
        "opening",
        (struct((pairs, width, LANES), f32), struct((pairs, heads, LANES), bf16)),
        (duo_hidden, bins, table_t, duo_logit_rescale[None], duo_logit_projector.T),
    )
    biases = [bias] + [shifted(bias, k) for k in (1, 2, 3)]
    wide = 4 * sites
    updated, factors = call(
        attention_kernel,
        "attention",
        (struct((lines, sites, feats), bf16), struct((lines, sites, 2 * outer_channels), f32)),
        (place, homolog_hidden, near, cross, far, flags, flags_near, flags_cross, flags_far)
        + tuple(biases)
        + (
            homolog_heeded_rescale[None],
            qkv_valve_projectors,
            heeded_exit_projector,
            dyadic_rescale[None],
            dyadic_factor_projector,
        ),
        [
            pltpu.VMEM((4, pairs * heads, LANES), f32),
            pltpu.VMEM((heads * sites, wide), f32),
            pltpu.VMEM((4, lines, LANES), f32),
            pltpu.VMEM((4, lines, sites, feats), bf16),
            pltpu.VMEM((4, lines, sites, feats), bf16),
            pltpu.VMEM((lines, sites, feats), bf16),
            pltpu.VMEM((lines, sites, feats), f32),
            pltpu.VMEM((lines, sites, feats), bf16),
        ],
        1,
    )
    factors = (factors * homolog_valid_flags.astype(f32)[..., None]).astype(bf16)
    left = factors[..., :outer_channels].reshape(lines, -1)
    right = jnp.swapaxes(factors[..., outer_channels:], 1, 2).reshape(lines, -1)
    left = jnp.concatenate([left, flags], axis=1)
    right = jnp.concatenate([right, flags], axis=1)
    lefts = [left] + [shifted(left, k) for k in (1, 2, 3)]

    def crossing(k):
        moves = []
        for a in range(4):
            for b in range(4):
                def spot(r, d):
                    return ((r // shape[2]) * shape[1] + d) * shape[2] + r % shape[2]
                moves.append((spot(a, b), spot(b ^ k, a)))
        return moves

    rights = [lax.ppermute(right, WHOLE, crossing(k)) for k in range(4)]
    entry_t = jnp.swapaxes(triad_entry_projectors, 1, 2)
    valve_t = jnp.swapaxes(triad_valve_projectors, 1, 2)
    exit_t = jnp.swapaxes(triad_exit_projectors, 1, 2)
    outer_t = jnp.transpose(
        dyadic_exit_projector.reshape(outer_channels, outer_channels, width), (2, 1, 0)
    ).reshape(width, -1)
    parcel_shape = struct((parts, pairs, 2 * chans, LANES), bf16)
    total = 4 * lines
    span = left.shape[1]
    state, parcel = call(
        outer_kernel,
        "outer",
        (struct(state.shape, f32), parcel_shape),
        (place, *lefts, *rights, state, outer_t, mask, triad_entry_rescales[:1], entry_t[0]),
        [
            pltpu.VMEM((4, lines, span), f32),
            pltpu.VMEM((4, lines, span), f32),
            pltpu.VMEM((pairs * outer_channels, 2 * total), bf16),
            pltpu.VMEM((outer_channels // 2, 2 * total, 2 * LANES), bf16),
            pltpu.VMEM((pairs, outer_channels, outer_channels, LANES), bf16),
            pltpu.VMEM((pairs, LANES), f32),
        ],
        1,
    )

    def exchange(values):
        return lax.all_to_all(values, WHOLE, split_axis=0, concat_axis=0, tiled=True)

    def triangle(parcel, incoming):
        product = call(
            functools.partial(product_kernel, incoming, shape),
            "product_in" if incoming else "product_out",
            struct((parts, pairs, chans, LANES), bf16),
            (exchange(parcel),),
            [
                pltpu.VMEM((2, pairs * 2 * chans, LANES), f32),
                pltpu.VMEM((chans, wide, wide), bf16),
                pltpu.VMEM((chans, wide, wide), bf16),
                pltpu.VMEM((parts, pairs * chans, LANES), f32),
            ],
        )
        return exchange(product)

    def weights(t):
        return (triad_entry_rescales[t : t + 1], valve_t[t], triad_exit_rescales[t : t + 1], exit_t[t])

    parcel = triangle(parcel, False)
    state, parcel = call(
        between_kernel,
        "between",
        (struct(state.shape, f32), parcel_shape),
        (parcel, state, *weights(0), mask, triad_entry_rescales[1:], entry_t[1]),
    )
    parcel = triangle(parcel, True)
    pair_out = call(
        closing_kernel, "closing", struct(duo_hidden.shape, bf16), (parcel, state, *weights(1))
    )
    return updated, pair_out


def solution(mesh):
    placed = (
        P(("groups", "dap"), ("branch", "tile"), None),
        P(("groups", "branch", "tile"), "dap", None),
        P(("groups", "dap"), ("branch", "tile")),
        P(("groups", "branch", "tile"), "dap"),
        P("groups"),
        P("groups"),
        P(),
        P(),
        P(),
        P(),
        P(),
        P(),
        P(),
        P(),
        P(),
        P(),
        P(),
        P(),
        P(),
        P(),
    )
    sizes = tuple(mesh.shape[axis] for axis in ("branch", "dap", "tile"))
    return jax.shard_map(
        fast_body if sizes == (2, 4, 2) else body,
        mesh=mesh,
        in_specs=placed,
        out_specs=(
            P(("groups", "dap"), ("branch", "tile"), None),
            P(("groups", "branch", "tile"), "dap", None),
        ),
        check_vma=False,
    )
```

```python
import functools

import jax
import jax.numpy as jnp
from jax import lax
from jax.experimental import pallas as pl
from jax.experimental.pallas import tpu as pltpu
from jax.sharding import PartitionSpec as P


REL_BINS = 66
LANES = 128
HEADS = 8
HALF = 64
VMEM_BYTES = 56 * 1024 * 1024
GROUP = 4
WHOLE = ("groups", "branch", "dap", "tile")


norm_eps = 1e-05
mask_big = 1000000000.0
count_eps = 0.001


def standardize_features(values, norm_gain, norm_axis):
    values = values.astype(jnp.float32)
    mean_val = jnp.mean(values, axis=norm_axis, keepdims=True)
    centred = values - mean_val
    spread = jnp.mean(centred * centred, axis=norm_axis, keepdims=True)
    return centred * lax.rsqrt(spread + norm_eps) * norm_gain


def threeway_update(
    duo_hidden_values, duo_valid_flags, norm_gain, w_in, w_gate, out_gain, w_out, incoming
):
    width_tri = w_in.shape[1] // 4
    tri_normed = standardize_features(duo_hidden_values, norm_gain, 2).astype(jnp.bfloat16)
    mapped_contents = jnp.einsum(
        "ijc,cd->idj", tri_normed, w_in, preferred_element_type=jnp.float32
    )
    mask_as_float = duo_valid_flags.astype(jnp.float32)[:, None, :]
    left_fac = (
        jax.nn.sigmoid(mapped_contents[:, width_tri : 2 * width_tri])
        * mapped_contents[:, :width_tri]
        * mask_as_float
    ).astype(jnp.bfloat16)
    right_fac = (
        jax.nn.sigmoid(mapped_contents[:, 3 * width_tri :])
        * mapped_contents[:, 2 * width_tri : 3 * width_tri]
        * mask_as_float
    ).astype(jnp.bfloat16)
    sigmoid_switches = jax.nn.sigmoid(
        jnp.einsum("ijc,cd->ijd", tri_normed, w_gate, preferred_element_type=jnp.float32)
    )
    left_split, right_split = (
        lax.all_to_all(left_fac, "dap", split_axis=1, concat_axis=2, tiled=True),
        lax.all_to_all(right_fac, "dap", split_axis=1, concat_axis=2, tiled=True),
    )
    if not incoming:
        product = jnp.einsum(
            "ick,jck->icj",
            left_split,
            lax.all_gather(right_split, ("branch", "tile"), axis=0, tiled=True),
            preferred_element_type=jnp.float32,
        )
    else:
        product = lax.psum_scatter(
            jnp.einsum(
                "kci,kcj->icj", left_split, right_split, preferred_element_type=jnp.float32
            ).astype(jnp.bfloat16),
            ("branch", "tile"),
            scatter_dimension=0,
            tiled=True,
        ).astype(jnp.float32)
    merged = lax.all_to_all(
        product.astype(jnp.bfloat16), "dap", split_axis=2, concat_axis=1, tiled=True
    )
    product_normed = standardize_features(merged, out_gain[:, None], 1).astype(jnp.bfloat16)
    update = jnp.einsum("icj,cz->ijz", product_normed, w_out, preferred_element_type=jnp.float32)
    return duo_hidden_values + sigmoid_switches * update


def body(
    homolog_hidden,
    duo_hidden,
    homolog_valid_flags,
    duo_valid_flags,
    polymer_labeling,
    monomer_serials,
    separation_bin_vectors,
    duo_logit_rescale,
    duo_logit_projector,
    homolog_heeded_rescale,
    qkv_valve_projectors,
    heeded_exit_projector,
    dyadic_rescale,
    dyadic_factor_projector,
    dyadic_exit_projector,
    triad_entry_rescales,
    triad_entry_projectors,
    triad_valve_projectors,
    triad_exit_rescales,
    triad_exit_projectors,
):
    lines_each_shard, sites_each_shard, lineup_feature_extent = homolog_hidden.shape
    columns_per_device = duo_hidden.shape[1]
    number_of_heads = duo_logit_projector.shape[1]
    head_channels = lineup_feature_extent // number_of_heads
    outer_channels = dyadic_factor_projector.shape[1] // 2
    row_start = lax.axis_index(("branch", "tile")) * sites_each_shard
    col_start = lax.axis_index("dap") * columns_per_device
    rel_reach = (REL_BINS - 2) // 2
    res_rows = lax.dynamic_slice_in_dim(monomer_serials, row_start, sites_each_shard)
    res_cols = lax.dynamic_slice_in_dim(monomer_serials, col_start, columns_per_device)
    chain_rows = lax.dynamic_slice_in_dim(polymer_labeling, row_start, sites_each_shard)
    chain_cols = lax.dynamic_slice_in_dim(polymer_labeling, col_start, columns_per_device)
    offset = jnp.clip(res_rows[:, None] - res_cols[None, :], -rel_reach, rel_reach) + rel_reach
    rel_bins = jnp.where(chain_rows[:, None] == chain_cols[None, :], offset, REL_BINS - 1)
    one_hot = (rel_bins[:, :, None] == jnp.arange(REL_BINS, dtype=jnp.int32)[None, None, :]).astype(
        jnp.bfloat16
    )
    duo_hidden_values = duo_hidden.astype(jnp.float32) + jnp.einsum(
        "ijb,bc->ijc", one_hot, separation_bin_vectors, preferred_element_type=jnp.float32
    )
    pair_normed = standardize_features(duo_hidden_values, duo_logit_rescale, 2).astype(jnp.bfloat16)
    local_bias = jnp.einsum(
        "ijc,ch->hij", pair_normed, duo_logit_projector, preferred_element_type=jnp.float32
    ).astype(jnp.bfloat16)
    row_bias = lax.all_gather(local_bias, "dap", axis=2, tiled=True)
    lineup_standardized = standardize_features(homolog_hidden, homolog_heeded_rescale, 2).astype(
        jnp.bfloat16
    )
    mapped_contents = jnp.einsum(
        "ezp,pb->ezb", lineup_standardized, qkv_valve_projectors, preferred_element_type=jnp.float32
    )
    asking_array = (mapped_contents[..., :lineup_feature_extent] * head_channels ** (-0.5)).astype(
        jnp.bfloat16
    )
    asking_array = asking_array.reshape(
        lines_each_shard, sites_each_shard, number_of_heads, head_channels
    )
    key_value_pairs = mapped_contents[
        ..., lineup_feature_extent : 3 * lineup_feature_extent
    ].astype(jnp.bfloat16)
    sigmoid_switches = jax.nn.sigmoid(mapped_contents[..., 3 * lineup_feature_extent :])
    mask_as_float = homolog_valid_flags.astype(jnp.bfloat16)
    run_max = jnp.full((lines_each_shard, number_of_heads, sites_each_shard), -jnp.inf, jnp.float32)
    run_sum = jnp.zeros((lines_each_shard, number_of_heads, sites_each_shard), jnp.float32)
    run_acc = jnp.zeros(
        (lines_each_shard, number_of_heads, sites_each_shard, head_channels), jnp.float32
    )
    key_value_slice = lax.all_gather(key_value_pairs, ("branch", "tile"), axis=1, tiled=True)
    mask_piece = lax.all_gather(mask_as_float, ("branch", "tile"), axis=1, tiled=True)
    slice_length = key_value_slice.shape[1]
    key_per_head = key_value_slice[..., :lineup_feature_extent].reshape(
        lines_each_shard, slice_length, number_of_heads, head_channels
    )
    value_per_head = key_value_slice[..., lineup_feature_extent:].reshape(
        lines_each_shard, slice_length, number_of_heads, head_channels
    )
    key_bias = row_bias.astype(jnp.float32)
    scores = jnp.einsum(
        "sihd,sjhd->shij", asking_array, key_per_head, preferred_element_type=jnp.float32
    )
    scores = (
        scores
        + key_bias[None]
        + ((mask_piece.astype(jnp.float32) - 1.0) * mask_big)[:, None, None, :]
    )
    new_max = jnp.max(scores, axis=-1)
    old_scale = jnp.exp(run_max - new_max)
    weights = jnp.exp(scores - new_max[..., None])
    run_sum = run_sum * old_scale + jnp.sum(weights, axis=-1)
    run_acc = run_acc * old_scale[..., None] + jnp.einsum(
        "shij,sjhd->shid",
        weights.astype(jnp.bfloat16),
        value_per_head,
        preferred_element_type=jnp.float32,
    )
    run_max, run_sum, run_acc = (new_max, run_sum, run_acc)
    focused_readout = run_acc / run_sum[..., None]
    focused_readout = jnp.transpose(focused_readout, (0, 2, 1, 3)).reshape(
        lines_each_shard, sites_each_shard, lineup_feature_extent
    )
    merged_focus_groups = (sigmoid_switches * focused_readout).astype(jnp.bfloat16)
    lineup_updated_state = (
        homolog_hidden.astype(jnp.float32)
        + jnp.einsum(
            "ezp,pb->ezb",
            merged_focus_groups,
            heeded_exit_projector,
            preferred_element_type=jnp.float32,
        )
    ).astype(jnp.bfloat16)
    outer_product_normalized = standardize_features(lineup_updated_state, dyadic_rescale, 2).astype(
        jnp.bfloat16
    )
    factors = (
        jnp.einsum(
            "ezp,pb->ezb",
            outer_product_normalized,
            dyadic_factor_projector,
            preferred_element_type=jnp.float32,
        )
        * homolog_valid_flags.astype(jnp.float32)[..., None]
    )
    left_flat = (
        factors[..., :outer_channels]
        .astype(jnp.bfloat16)
        .reshape(lines_each_shard, sites_each_shard * outer_channels)
    )
    right_flat = (
        factors[..., outer_channels:]
        .astype(jnp.bfloat16)
        .reshape(lines_each_shard, sites_each_shard * outer_channels)
    )
    right_all, mask_all = (
        lax.all_gather(right_flat, ("branch", "tile"), axis=1, tiled=True),
        lax.all_gather(mask_as_float, ("branch", "tile"), axis=1, tiled=True),
    )
    total_res = mask_all.shape[1]
    right_all = right_all.reshape(lines_each_shard, total_res, outer_channels)
    right_factor_rows, mask_right = (
        lax.all_to_all(right_all, "dap", split_axis=1, concat_axis=0, tiled=True),
        lax.all_to_all(mask_all, "dap", split_axis=1, concat_axis=0, tiled=True),
    )
    left_factor_rows, mask_rows = (
        lax.all_gather(left_flat, "dap", axis=0, tiled=True),
        lax.all_gather(mask_as_float, "dap", axis=0, tiled=True),
    )
    alignment_rows = left_factor_rows.shape[0]
    left_factor_rows = left_factor_rows.reshape(alignment_rows, sites_each_shard, outer_channels)
    counts = jnp.einsum("si,sj->ij", mask_rows, mask_right, preferred_element_type=jnp.float32)
    outer_prod = jnp.einsum(
        "sic,sjd->ijcd", left_factor_rows, right_factor_rows, preferred_element_type=jnp.float32
    ).astype(jnp.bfloat16)
    outer_prod = outer_prod.reshape(
        sites_each_shard, columns_per_device, outer_channels * outer_channels
    )
    update = jnp.einsum(
        "ijk,kz->ijz", outer_prod, dyadic_exit_projector, preferred_element_type=jnp.float32
    )
    duo_hidden_values = duo_hidden_values + update / (count_eps + counts)[..., None]
    for threefold_module in range(2):
        duo_hidden_values = threeway_update(
            duo_hidden_values,
            duo_valid_flags,
            triad_entry_rescales[threefold_module],
            triad_entry_projectors[threefold_module],
            triad_valve_projectors[threefold_module],
            triad_exit_rescales[threefold_module],
            triad_exit_projectors[threefold_module],
            threefold_module == 1,
        )
    return (lineup_updated_state, duo_hidden_values.astype(jnp.bfloat16))


def standardize_sublanes(values, gain):
    mean_val = jnp.mean(values, axis=0, keepdims=True)
    centred = values - mean_val
    spread = jnp.mean(centred * centred, axis=0, keepdims=True)
    return (centred * lax.rsqrt(spread + norm_eps) * gain).astype(jnp.bfloat16)


def standardize_lanes(values, gain):
    mean_val = jnp.mean(values, axis=-1, keepdims=True)
    centred = values - mean_val
    spread = jnp.mean(centred * centred, axis=-1, keepdims=True)
    return (centred * lax.rsqrt(spread + norm_eps) * gain).astype(jnp.bfloat16)


def matmul(a, b, dims=((1,), (0,))):
    return lax.dot_general(a, b, (dims, ((), ())), preferred_element_type=jnp.float32)


def swap_halves(first, second):
    low = lax.broadcasted_iota(jnp.int32, first.shape, first.ndim - 1) < HALF
    turned_first = pltpu.roll(first, HALF, first.ndim - 1)
    turned_second = pltpu.roll(second, HALF, second.ndim - 1)
    return jnp.where(low, first, turned_second), jnp.where(low, turned_first, second)


def column_of(row):
    return jnp.broadcast_to(row, (row.shape[1], row.shape[1])).T


def opening_state(first, row_of, codes, table_t):
    pairs = codes.shape[0]
    block = jnp.concatenate(
        [row_of(first + p + half * pairs) for p in range(GROUP) for half in range(2)], axis=0
    )
    levels = jnp.concatenate(
        [codes[pl.ds(first + p, 1), :] & (LANES - 1) for p in range(GROUP)], axis=1
    )
    one_hot = lax.broadcasted_iota(jnp.int32, (table_t.shape[1], GROUP * LANES), 0) == levels
    unit = lax.broadcasted_iota(jnp.int32, (LANES, LANES), 0) == lax.broadcasted_iota(
        jnp.int32, (LANES, LANES), 1
    )
    turned = matmul(unit.astype(jnp.float32).astype(jnp.bfloat16), block, ((1,), (1,)))
    return turned + matmul(table_t, one_hot.astype(jnp.float32).astype(jnp.bfloat16))


def transposed(value):
    return value.astype(jnp.float32).T.astype(jnp.bfloat16)


def opening_kernel(duo, codes, table, gain, projector, bias):
    table_t, projector_t = transposed(table[...]), transposed(projector[...])
    gain_col = column_of(gain[...])
    gain_col = jnp.concatenate([gain_col] * GROUP, axis=1)
    pairs = codes.shape[0]

    def step(q, carry):
        value = opening_state(GROUP * q, lambda i: duo[i], codes, table_t)
        normed = standardize_sublanes(value, gain_col)
        part = matmul(projector_t, normed).astype(jnp.bfloat16)
        for p in range(GROUP):
            bias[GROUP * q + p] = part[:, p * LANES : (p + 1) * LANES]
        return carry

    lax.fori_loop(0, pairs // GROUP, step, 0)


def project_kernel(
    place, own, near, cross, far, gain, projectors, keys, vals, query, gate, flag_all
):
    row = place[0]
    feats = own.shape[2]
    lines, sites = query.shape[:2]
    width = feats // HEADS
    for k, piece in enumerate((own, near, cross, far)):
        flag_all[row ^ k] = piece[:, sites : sites + 8, :LANES].astype(jnp.float32)[:, 0]
        normed = standardize_lanes(
            piece[:, :sites].astype(jnp.float32).reshape(lines * sites, feats), gain[...]
        )
        both = matmul(normed, projectors[:, feats : 3 * feats]).astype(jnp.bfloat16)
        keys[row ^ k] = both[:, :feats].reshape(lines, sites, feats)
        vals[row ^ k] = both[:, feats:].reshape(lines, sites, feats)
        if k == 0:
            query[...] = (
                (matmul(normed, projectors[:, :feats]) * width ** (-0.5))
                .astype(jnp.bfloat16)
                .reshape(lines, sites, feats)
            )
            gate[...] = jax.nn.sigmoid(matmul(normed, projectors[:, 3 * feats :])).reshape(
                lines, sites, feats
            )


def attention_kernel(
    place, own, keys, vals, query, gate, flag_all, bias_0, bias_1, bias_2, bias_3,
    exit_projector, outer_gain, factor_projector,
    updated, factors,
    bias_in, bias_all, mixed,
):
    col = place[1]
    lines, sites, feats = own.shape
    heads = bias_0.shape[1]
    width = feats // heads
    pairs = bias_0.shape[0]
    for k, piece in enumerate((bias_0, bias_1, bias_2, bias_3)):
        bias_in[col ^ k] = piece[...].astype(jnp.float32).reshape(pairs * heads, LANES)
    for head in range(heads):
        for pair in range(2):
            first = bias_in[2 * pair, pl.ds(head, pairs, stride=heads), :]
            second = bias_in[2 * pair + 1, pl.ds(head, pairs, stride=heads), :]
            upper, lower = swap_halves(first, second)
            bias_all[head * sites : head * sites + pairs, pair * LANES : (pair + 1) * LANES] = upper
            bias_all[head * sites + pairs : (head + 1) * sites, pair * LANES : (pair + 1) * LANES] = lower
    lane_head = lax.broadcasted_iota(jnp.int32, (sites, feats), 1) // width

    def step(s, carry):
        q = query[s].astype(jnp.float32)
        q_all = jnp.concatenate(
            [jnp.where(lane_head == h, q, 0.0) for h in range(heads)], axis=0
        ).astype(jnp.bfloat16)
        k_all = jnp.concatenate([keys[b, s] for b in range(4)], axis=0)
        v_all = jnp.concatenate([vals[b, s] for b in range(4)], axis=0)
        flag_rows = [flag_all[b, pl.ds(s, 1), :] for b in range(4)]
        flag_row = jnp.concatenate(
            [
                swap_halves(flag_rows[0], flag_rows[1])[0],
                swap_halves(flag_rows[2], flag_rows[3])[0],
            ],
            axis=1,
        )
        scores = matmul(q_all, k_all, ((1,), (1,))) + bias_all[...]
        scores = scores + (flag_row - 1.0) * mask_big
        weights = jnp.exp(scores - jnp.max(scores, axis=-1, keepdims=True))
        total = jnp.sum(weights, axis=-1, keepdims=True)
        read = matmul(weights.astype(jnp.bfloat16), v_all) / total
        picked = jnp.zeros((sites, feats), jnp.float32)
        for h in range(heads):
            picked = jnp.where(lane_head == h, read[h * sites : (h + 1) * sites], picked)
        mixed[s] = (gate[s] * picked).astype(jnp.bfloat16)
        return carry

    lax.fori_loop(0, lines, step, 0)
    new = own[...].astype(jnp.float32).reshape(lines * sites, feats) + matmul(
        mixed[...].reshape(lines * sites, feats), exit_projector[...]
    )
    new = new.astype(jnp.bfloat16)
    updated[...] = new.reshape(lines, sites, feats)
    normed = standardize_lanes(new.astype(jnp.float32), outer_gain[...])
    factors[...] = matmul(normed, factor_projector[...]).reshape(lines, sites, -1)


def gather_pairs(ref, first):
    return jnp.concatenate([ref[first + p] for p in range(GROUP)], axis=1)


def scatter_pairs(ref, first, value):
    for p in range(GROUP):
        ref[first + p] = value[:, p * LANES : (p + 1) * LANES]


def mask_row(codes, first):
    row = jnp.concatenate([codes[pl.ds(first + p, 1), :] for p in range(GROUP)], axis=1)
    return (row // LANES).astype(jnp.float32)


def wide_gain(gain, turn=0):
    return jnp.concatenate([column_of(gain[turn : turn + 1])] * GROUP, axis=1)


def prepare_kernel(entry, valve, leave, outer, entry_t, valve_t, exit_t, outer_t, wide):
    for turn in range(2):
        entry_t[turn] = transposed(entry[turn])
        valve_t[turn] = transposed(valve[turn])
        exit_t[turn] = transposed(leave[turn])
    wide[...] = outer[...].astype(jnp.float32)
    feats = outer_t.shape[1] // 32
    for d in range(feats):
        part = wide[pl.ds(d, 32, stride=feats), :]
        wide_t = part.T
        outer_t[:, d * 32 : (d + 1) * 32] = wide_t.astype(jnp.bfloat16)


def send_factors(turn, value, first, entry_t, gain_col, flag, parcel):
    normed = standardize_sublanes(value, gain_col)
    width = value.shape[0]
    parts = parcel.shape[0]
    sides = []
    for side in range(2):
        mapped = matmul(entry_t[turn, 2 * side * width : 2 * (side + 1) * width, :], normed)
        factor = jax.nn.sigmoid(mapped[width:]) * mapped[:width] * flag
        sides.append(factor.reshape(parts, -1, GROUP * LANES))
    both = jnp.concatenate(sides, axis=1).astype(jnp.bfloat16)
    for p in range(GROUP):
        parcel[:, first + p] = both[:, :, p * LANES : (p + 1) * LANES]


def outer_kernel(
    place, left_0, left_1, left_2, left_3, right_0, right_1, right_2, right_3,
    duo, duo_0, duo_1, duo_2, codes, table, outer_t, gain, entry_t,
    new_state, parcel,
    left_all, right_all, left_t, right_wide, outer, scale,
):
    row, col = place[0], place[1]
    lines = left_0.shape[0]
    pairs = codes.shape[0]
    for k, piece in enumerate((left_0, left_1, left_2, left_3)):
        left_all[col ^ k] = piece[...].astype(jnp.float32)
    for k, piece in enumerate((right_0, right_1, right_2, right_3)):
        right_all[row ^ k] = piece[...].astype(jnp.float32)
    total = left_all.shape[0] * lines
    span = left_all.shape[2] - LANES
    left = left_all[...].reshape(total, span + LANES)
    right = right_all[...].reshape(total, span + LANES)
    stacked = jnp.concatenate([left[:, : span // 2], left[:, span // 2 : span]], axis=0)
    left_t[...] = stacked.T.astype(jnp.bfloat16)
    tiles = span // LANES
    low = lax.broadcasted_iota(jnp.int32, (total, LANES), 1) < HALF
    for t in range(tiles):
        piece = right[:, t * LANES : (t + 1) * LANES]
        turned = pltpu.roll(piece, HALF, 1)
        first = jnp.concatenate([jnp.where(low, piece, 0.0), jnp.where(low, 0.0, turned)], axis=0)
        second = jnp.concatenate([jnp.where(low, turned, 0.0), jnp.where(low, 0.0, piece)], axis=0)
        right_wide[t] = jnp.concatenate([first, second], axis=1).astype(jnp.bfloat16)
    flags_left = left[:, span:]
    flags_left = jnp.concatenate([flags_left, pltpu.roll(flags_left, LANES - HALF // 2, 1)], axis=0)
    flags_left = flags_left.T[:pairs].astype(jnp.bfloat16)
    flags_right = right[:, span:]
    flags_right = jnp.concatenate(
        [jnp.where(low, flags_right, 0.0), jnp.where(low, 0.0, pltpu.roll(flags_right, HALF, 1))],
        axis=0,
    ).astype(jnp.bfloat16)
    scale[...] = 1.0 / (count_eps + matmul(flags_left, flags_right))
    chans = left_t.shape[0] // pairs

    def expand(t, carry):
        tile = matmul(left_t[...], right_wide[t])
        for half in range(2):
            outer[:, 2 * t + half] = (
                tile[:, half * LANES : (half + 1) * LANES]
                .reshape(pairs, chans, LANES)
                .astype(jnp.bfloat16)
            )
        return carry

    lax.fori_loop(0, tiles, expand, 0)
    gain_col = wide_gain(gain)
    table_t = transposed(table[...])
    rows = [(piece, i) for piece in (duo_0, duo_1, duo_2) for i in range(piece.shape[0])]

    def row_of(i):
        piece, place_in = rows[i]
        stays = jnp.full(piece.shape[1:], place[2], jnp.int32) > 0
        return jnp.where(
            stays, duo[i].astype(jnp.float32), piece[place_in].astype(jnp.float32)
        ).astype(jnp.bfloat16)

    for first in range(0, pairs, GROUP):
        flat = jnp.concatenate(
            [outer[first + p].reshape(-1, LANES) for p in range(GROUP)], axis=1
        )
        factor = jnp.concatenate([scale[pl.ds(first + p, 1), :] for p in range(GROUP)], axis=1)
        value = opening_state(first, row_of, codes, table_t) + matmul(outer_t[...], flat) * factor
        scatter_pairs(new_state, first, value)
        send_factors(0, value, first, entry_t, gain_col, mask_row(codes, first), parcel)


def product_kernel(incoming, shape, parcel, *refs):
    *results, buffer, left, right, wide = refs
    branches, columns, tiles = shape
    pairs, both = parcel.shape[1], parcel.shape[2]
    chans = both // 2
    sites = 2 * pairs
    for b in range(branches):
        for t in range(tiles):
            row = b * tiles + t
            for pair in range(columns // 2):
                for e in range(2):
                    src = (b * columns + 2 * pair + e) * tiles + t
                    buffer[e] = parcel[src].astype(jnp.float32).reshape(pairs * both, LANES)
                for c in range(both):
                    upper, lower = swap_halves(
                        buffer[0, pl.ds(c, pairs, stride=both), :],
                        buffer[1, pl.ds(c, pairs, stride=both), :],
                    )
                    target = left if c < chans else right
                    lanes = slice(pair * LANES, (pair + 1) * LANES)
                    target[c % chans, row * sites : row * sites + pairs, lanes] = upper.astype(
                        jnp.bfloat16
                    )
                    target[c % chans, row * sites + pairs : (row + 1) * sites, lanes] = lower.astype(
                        jnp.bfloat16
                    )
    dims = ((0,), (0,)) if incoming else ((1,), (1,))
    for c in range(chans):
        value = matmul(left[c], right[c], dims)
        for b in range(branches):
            for t in range(tiles):
                row = b * tiles + t
                for pair in range(columns // 2):
                    lanes = slice(pair * LANES, (pair + 1) * LANES)
                    halves = swap_halves(
                        value[row * sites : row * sites + pairs, lanes],
                        value[row * sites + pairs : (row + 1) * sites, lanes],
                    )
                    for e in range(2):
                        dst = (b * columns + 2 * pair + e) * tiles + t
                        wide[dst, pl.ds(c, pairs, stride=chans), :] = halves[e]
    first = 0
    for result in results:
        rows = result.shape[1] * chans
        result[...] = wide[:, first : first + rows].reshape(result.shape).astype(jnp.bfloat16)
        first += rows


def merged_update(turn, first, parcel, state, gain_in, valve_t, gain_out, exit_t, offset=0):
    value = gather_pairs(state, offset + first)
    normed = standardize_sublanes(value, gain_in)
    switch = jax.nn.sigmoid(matmul(valve_t[turn], normed))
    product = jnp.concatenate(
        [
            parcel[:, first + p].astype(jnp.float32).reshape(value.shape[0], LANES)
            for p in range(GROUP)
        ],
        axis=1,
    )
    update = matmul(exit_t[turn], standardize_sublanes(product, gain_out))
    return value + switch * update


def between_kernel(
    parcel, state, gain_in, valve_t, gain_out, exit_t, codes, entry_t, new_state, new_parcel
):
    gains = [wide_gain(gain_in), wide_gain(gain_out), wide_gain(gain_in, 1)]

    def step(q, carry):
        first = GROUP * q
        value = merged_update(0, first, parcel, state, gains[0], valve_t, gains[1], exit_t)
        scatter_pairs(new_state, first, value)
        send_factors(1, value, first, entry_t, gains[2], mask_row(codes, first), new_parcel)
        return carry

    lax.fori_loop(0, state.shape[0] // GROUP, step, 0)


def closing_kernel(offset, parcel, state, gain_in, valve_t, gain_out, exit_t, *outs):
    gains = [wide_gain(g, 1) for g in (gain_in, gain_out)]
    pairs = parcel.shape[1]
    cols = outs[0].shape[1]
    places = [(out, i) for out in outs for i in range(out.shape[0])]
    for first in range(0, pairs, GROUP):
        value = merged_update(
            1, first, parcel, state, gains[0], valve_t, gains[1], exit_t, offset
        )
        for p in range(GROUP):
            part = value[:, p * LANES : (p + 1) * LANES].T.astype(jnp.bfloat16)
            for half in range(2):
                out, i = places[first + p + half * pairs]
                out[i] = part[half * cols : (half + 1) * cols]


def call(kernel, out_shape, args, scratch=(), scalars=0):
    spec = pl.BlockSpec(memory_space=pltpu.VMEM)
    return pl.pallas_call(
        kernel,
        out_shape=out_shape,
        in_specs=[pl.BlockSpec(memory_space=pltpu.SMEM)] * scalars
        + [spec] * (len(args) - scalars),
        out_specs=jax.tree.map(lambda _: spec, out_shape),
        scratch_shapes=scratch,
        compiler_params=pltpu.CompilerParams(vmem_limit_bytes=VMEM_BYTES),
    )(*args)


def fast_body(*args):
    return fast_program(*args)


def fast_program(
    homolog_hidden,
    duo_hidden,
    homolog_valid_flags,
    duo_valid_flags,
    polymer_labeling,
    monomer_serials,
    separation_bin_vectors,
    duo_logit_rescale,
    duo_logit_projector,
    homolog_heeded_rescale,
    qkv_valve_projectors,
    heeded_exit_projector,
    dyadic_rescale,
    dyadic_factor_projector,
    dyadic_exit_projector,
    triad_entry_rescales,
    triad_entry_projectors,
    triad_valve_projectors,
    triad_exit_rescales,
    triad_exit_projectors,
):
    f32, bf16 = jnp.float32, jnp.bfloat16
    struct = jax.ShapeDtypeStruct
    lines, sites, feats = homolog_hidden.shape
    columns, width = duo_hidden.shape[1:]
    heads = duo_logit_projector.shape[1]
    outer_channels = dyadic_factor_projector.shape[1] // 2
    crops, *shape = (lax.axis_size(axis) for axis in WHOLE)
    parts = shape[0] * shape[1] * shape[2]

    def number(crop, r, d):
        return ((crop * shape[0] + r // shape[2]) * shape[1] + d) * shape[2] + r % shape[2]

    def hosted(crop, r, d):
        if d // 2 == crop:
            return number(crop, r, d)
        return number(1 - crop, r, d ^ 2)

    blocks = [(g, r, d) for g in range(crops) for r in range(shape[0] * shape[2]) for d in range(shape[1])]
    foreign = [b for b in blocks if b[2] // 2 != b[0]]
    cubes = [
        [hosted(g, b * shape[2] + t, d) for b in range(shape[0]) for d in range(shape[1]) for t in range(shape[2])]
        for g in range(crops)
    ]
    pairs = sites // 2
    chans = width // parts
    row = lax.axis_index(("branch", "tile"))
    col = lax.axis_index("dap")
    at_home = lax.axis_index("groups") == col // 2
    place = jnp.stack([row, col]).astype(jnp.int32)
    work_place = jnp.stack([row, jnp.where(at_home, col, col ^ 2), at_home]).astype(jnp.int32)
    flip = [(0, 1), (1, 0)]
    home = [(number(*b), hosted(*b)) for b in blocks]

    def hops(blocks_moved, outward, crop_first):
        moves = []
        for g, r, d in blocks_moved:
            ends = [number(g, r, d), hosted(g, r, d)]
            middle = number(1 - g, r, d) if outward else number(g, r, d ^ 2)
            path = [ends[0], middle, ends[1]] if outward else [ends[1], middle, ends[0]]
            moves.append((path[0], path[1]) if crop_first else (path[1], path[2]))
        return moves

    flags = jnp.pad(homolog_valid_flags.astype(bf16), ((0, 0), (0, LANES - sites)))
    packed = jnp.concatenate(
        [homolog_hidden, jnp.pad(flags[:, None, :], ((0, 0), (0, 7), (0, feats - LANES)))], axis=1
    )
    near = lax.ppermute(packed, "tile", flip)
    cross = lax.ppermute(packed, "branch", flip)
    far = lax.ppermute(near, "branch", flip)
    cuts = (5 * sites // 16, 21 * sites // 32)
    away = [(number(*b), hosted(*b)) for b in foreign]
    duo_first = lax.ppermute(duo_hidden[: cuts[0]], WHOLE, away)
    duo_relay = lax.ppermute(duo_hidden[cuts[0] : cuts[1]], WHOLE, hops(foreign, True, True))
    duo_last = lax.ppermute(duo_hidden[cuts[1] :], WHOLE, away)
    duo_relay = lax.ppermute(duo_relay, WHOLE, hops(foreign, True, False))

    rel_reach = (REL_BINS - 2) // 2
    res_rows = lax.dynamic_slice_in_dim(monomer_serials, row * sites, sites)
    res_cols = lax.dynamic_slice_in_dim(monomer_serials, col * columns, columns)
    chain_rows = lax.dynamic_slice_in_dim(polymer_labeling, row * sites, sites)
    chain_cols = lax.dynamic_slice_in_dim(polymer_labeling, col * columns, columns)
    offset = jnp.clip(res_rows[:, None] - res_cols[None, :], -rel_reach, rel_reach) + rel_reach
    bins = jnp.where(chain_rows[:, None] == chain_cols[None, :], offset, REL_BINS - 1)
    codes = bins + LANES * duo_valid_flags
    codes = jnp.concatenate([codes[:pairs], codes[pairs:]], axis=1)
    work_codes = lax.ppermute(codes, WHOLE, home)

    bias = call(
        opening_kernel,
        struct((pairs, heads, LANES), bf16),
        (duo_hidden, codes, separation_bin_vectors, duo_logit_rescale[None], duo_logit_projector),
    )
    biases = [bias] + [
        lax.ppermute(bias, "dap", [(i, i ^ k) for i in range(shape[1])]) for k in (1, 2, 3)
    ]
    wide = 4 * sites
    keys, vals, query, gate, flag_all = call(
        project_kernel,
        (
            struct((4, lines, sites, feats), bf16),
            struct((4, lines, sites, feats), bf16),
            struct((lines, sites, feats), bf16),
            struct((lines, sites, feats), f32),
            struct((4, lines, LANES), f32),
        ),
        (place, packed, near, cross, far, homolog_heeded_rescale[None], qkv_valve_projectors),
        scalars=1,
    )
    updated, factors = call(
        attention_kernel,
        (struct((lines, sites, feats), bf16), struct((lines, sites, 2 * outer_channels), f32)),
        (place, homolog_hidden, keys, vals, query, gate, flag_all, *biases)
        + (heeded_exit_projector, dyadic_rescale[None], dyadic_factor_projector),
        [
            pltpu.VMEM((4, pairs * heads, LANES), f32),
            pltpu.VMEM((heads * sites, wide), f32),
            pltpu.VMEM((lines, sites, feats), bf16),
        ],
        1,
    )
    entry_t, valve_t, exit_t, outer_t = call(
        prepare_kernel,
        (
            struct((2, 4 * width, width), bf16),
            struct((2, width, width), bf16),
            struct((2, width, width), bf16),
            struct((width, outer_channels * outer_channels), bf16),
        ),
        (triad_entry_projectors, triad_valve_projectors, triad_exit_projectors, dyadic_exit_projector),
        [pltpu.VMEM(dyadic_exit_projector.shape, f32)],
    )
    factors = (factors * homolog_valid_flags.astype(f32)[..., None]).astype(bf16)
    left = factors[..., :outer_channels].reshape(lines, -1)
    right = jnp.swapaxes(factors[..., outer_channels:], 1, 2).reshape(lines, -1)
    left = jnp.concatenate([left, flags], axis=1)
    right = jnp.concatenate([right, flags], axis=1)
    lefts = [
        lax.ppermute(left, WHOLE, [(number(*b), hosted(b[0], b[1], b[2] ^ k)) for b in blocks])
        for k in range(4)
    ]
    rights = [
        lax.ppermute(right, WHOLE, [(number(*b), hosted(b[0], b[2] ^ k, b[1])) for b in blocks])
        for k in range(4)
    ]
    parcel_shape = struct((parts, pairs, 2 * chans, LANES), bf16)
    total = 4 * lines
    span = left.shape[1]
    state, parcel = call(
        outer_kernel,
        (struct((pairs, width, LANES), f32), parcel_shape),
        (
            work_place, *lefts, *rights, duo_hidden, duo_first, duo_relay, duo_last, work_codes,
            separation_bin_vectors, outer_t, triad_entry_rescales, entry_t,
        ),
        [
            pltpu.VMEM((4, lines, span), f32),
            pltpu.VMEM((4, lines, span), f32),
            pltpu.VMEM((pairs * outer_channels, 2 * total), bf16),
            pltpu.VMEM((outer_channels // 2, 2 * total, 2 * LANES), bf16),
            pltpu.VMEM((pairs, outer_channels, outer_channels, LANES), bf16),
            pltpu.VMEM((pairs, LANES), f32),
        ],
        1,
    )

    def exchange(values):
        return lax.all_to_all(
            values, WHOLE, split_axis=0, concat_axis=0, tiled=True, axis_index_groups=cubes
        )

    def triangle(parcel, incoming, pieces):
        products = call(
            functools.partial(product_kernel, incoming, shape),
            (struct((parts, pairs // pieces, chans, LANES), bf16),) * pieces,
            (exchange(parcel),),
            [
                pltpu.VMEM((2, pairs * 2 * chans, LANES), f32),
                pltpu.VMEM((chans, wide, wide), bf16),
                pltpu.VMEM((chans, wide, wide), bf16),
                pltpu.VMEM((parts, pairs * chans, LANES), f32),
            ],
        )
        return [exchange(product) for product in products]

    weights = (triad_entry_rescales, valve_t, triad_exit_rescales, exit_t)
    (parcel,) = triangle(parcel, False, 1)
    state, parcel = call(
        between_kernel,
        (struct(state.shape, f32), parcel_shape),
        (parcel, state, *weights, work_codes, entry_t),
    )
    pieces = 2
    early, late = hops(foreign, False, True), hops(foreign, False, False)
    back = [(hosted(*b), number(*b)) for b in foreign]
    rows = sites // pieces
    sizes = (3 * rows // 8, 5 * rows // 8)
    finished = []
    for piece, parcel in enumerate(triangle(parcel, True, pieces)):
        results = call(
            functools.partial(closing_kernel, piece * pairs // pieces),
            tuple(struct((size, columns, width), bf16) for size in sizes),
            (parcel, state, *weights),
        )
        relay = lax.ppermute(results[0], WHOLE, early)
        direct = lax.ppermute(results[1], WHOLE, back)
        relay = lax.ppermute(relay, WHOLE, late)
        whole = jnp.concatenate(
            [jnp.where(at_home, results[0], relay), jnp.where(at_home, results[1], direct)], axis=0
        )
        finished.append(whole)
    pair_out = jnp.concatenate(
        [piece[half * rows // 2 : (half + 1) * rows // 2] for half in range(2) for piece in finished],
        axis=0,
    )
    return updated, pair_out


def solution(mesh):
    placed = (
        P(("groups", "dap"), ("branch", "tile"), None),
        P(("groups", "branch", "tile"), "dap", None),
        P(("groups", "dap"), ("branch", "tile")),
        P(("groups", "branch", "tile"), "dap"),
        P("groups"),
        P("groups"),
        P(),
        P(),
        P(),
        P(),
        P(),
        P(),
        P(),
        P(),
        P(),
        P(),
        P(),
        P(),
        P(),
        P(),
    )
    sizes = tuple(mesh.shape[axis] for axis in WHOLE)
    fast = sizes == (2, 2, 4, 2)
    return jax.shard_map(
        fast_body if fast else body,
        mesh=mesh,
        in_specs=placed,
        out_specs=(
            P(("groups", "dap"), ("branch", "tile"), None),
            P(("groups", "branch", "tile"), "dap", None),
        ),
        check_vma=False,
    )
```
